128 devices in a mesh: grp: 8 (over y_lo, z), dev: 16 (over y_hi, x, core).
Axes of the slice: x: 4, y: 4 (y_hi: 2, y_lo: 2; y = y_hi * 2 + y_lo), z: 4, core: 2. Of those that a mesh axis runs over, the one named last changes fastest.
Arguments:
- queries: bfloat16 [131072, 2048], P(('grp', 'dev')), may hold values from -48 to 48
- key_rows: bfloat16 [131072, 2048], P(('grp', 'dev')), may hold values from -6 to 6
- value_rows: bfloat16 [131072, 2048], P(('grp', 'dev')), may hold values from -6 to 6
Outputs:
- attended: bfloat16 [131072, 2048], P(('grp', 'dev'))
The draws below stay inside these ranges and needn't reach their ends.
All inputs are finite; a program needn't handle non-finite values.
Results may differ from the reference program's by a relative error of at most 0.0026.
Values may be sent and summed in bfloat16 or wider, within the bound.
A program may use at most 256 MiB of HBM per device.

```python
import math
import jax
import jax.numpy as jnp
import numpy as np
from jax import lax

D = 2048
H = 16
HD = 128
TOK_DEV = 1024
SEQUENCE_TOKENS = 131072
MIDDLE_SEGMENT = 16384
MIDDLE_DILATION = 16
GLOBAL_DILATION = 128


def draw_pair(key):
    query_key = jax.random.fold_in(key, 101)
    row_key = jax.random.fold_in(key, 202)
    query_draw = 4.0 * jax.random.truncated_normal(query_key, -6.0, 6.0, (SEQUENCE_TOKENS, D), jnp.float32)
    key_sampler = jax.random.truncated_normal(row_key, -6.0, 6.0, (SEQUENCE_TOKENS, D), jnp.float32)
    return (query_draw, key_sampler)


def draw_queries(key, part):
    return draw_pair(key)[0].astype(jnp.bfloat16)


def draw_key_rows(key, part):
    return draw_pair(key)[1].astype(jnp.bfloat16)


def steps_of(own_key, shape, pieces, smallest, largest):
    def one(axis_at, shards_of):
        steps = jax.random.uniform(jax.random.fold_in(jax.random.fold_in(own_key, 6), axis_at), (shards_of,), jnp.float32, smallest / len(pieces), largest / len(pieces))
        return jnp.repeat(jnp.exp(steps), shape[axis_at] // shards_of).reshape((-1,) + (1,) * (len(shape) - axis_at - 1))

    gain = one(*pieces[0])
    for cut in pieces[1:]:
        gain = gain * one(*cut)
    return gain


def bell_draw(rng, shape, deviation, bound, cuts=(), kind=jnp.bfloat16):
    entries = jax.random.normal(rng, shape, jnp.float32) * deviation
    if len(cuts) > 0:
        entries = steps_of(rng, shape, cuts, -0.22, 0.18) * entries
    return jnp.clip(entries, min=-bound, max=bound).astype(kind)


def setup_inputs(seed: int = 0) -> dict:
    seeds = jax.random.split(jax.random.key(seed), 4)
    return {
        "queries": draw_queries(jax.random.fold_in(seeds[3], 71), 0),
        "key_rows": draw_key_rows(jax.random.fold_in(seeds[3], 71), 0),
        "value_rows": bell_draw(seeds[2], (SEQUENCE_TOKENS, D), 1.0, 6.0, ((0, 128),)),
    }


def attend(query_rows, key_part, value_part):
    score_scale = 1.0 / math.sqrt(query_rows.shape[-1])
    scores = jnp.einsum('qhe,khe->hqk', query_rows.astype(jnp.float32), key_part.astype(jnp.float32)) * score_scale
    maxima = lax.optimization_barrier(jnp.max(scores, axis=2))
    weights = jnp.exp(scores - maxima[:, :, None])
    totals = lax.optimization_barrier(jnp.sum(weights, axis=2))
    rounded = lax.optimization_barrier(weights.astype(jnp.bfloat16)).astype(jnp.float32)
    summed = jnp.einsum('hqk,khe->qhe', rounded, value_part.astype(jnp.float32))
    return (maxima.T, totals.T, summed)

def picked_rows(source, dilation):
    head_ids = np.arange(H)
    shaped = source.reshape(source.shape[0] // dilation, dilation, H, HD)
    return shaped[:, head_ids % dilation, head_ids, :]

def gap_between(maxima, totals, summed, dilation):
    select_mask = jnp.asarray(np.arange(dilation)[:, None] == (np.arange(H) % dilation)[None, :])
    full_max = jnp.where(select_mask[None], maxima[:, None, :], -jnp.inf).reshape(-1, H)
    full_tot = jnp.where(select_mask[None], totals[:, None, :], 0.0).reshape(-1, H)
    full_sum = jnp.where(select_mask[None, :, :, None], summed[:, None], 0.0).reshape(-1, H, HD)
    return (full_max, full_tot, full_sum)

def combine(branch_list):
    highest = branch_list[0][0]
    for branch in branch_list[1:]:
        highest = jnp.maximum(highest, branch[0])
    numerator = jnp.zeros_like(branch_list[0][2])
    denominator = jnp.zeros_like(branch_list[0][1])
    for branch in branch_list:
        factor = jnp.exp(branch[0] - highest)
        denominator = denominator + branch[1] * factor
        numerator = numerator + branch[2] * factor[:, :, None]
    return numerator / denominator[:, :, None]

def reference(queries, key_rows, value_rows):
    query_per_head = queries.reshape(SEQUENCE_TOKENS, H, HD)
    key_per_head = key_rows.reshape(SEQUENCE_TOKENS, H, HD)
    value_per_head = value_rows.reshape(SEQUENCE_TOKENS, H, HD)

    def branch_softmax_totals(segments, dilation):
        triple = tuple((picked_rows(source, dilation).reshape(segments, -1, H, HD) for source in (query_per_head, key_per_head, value_per_head)))
        maxima, totals, summed = lax.map(lambda chosen: attend(chosen[0], chosen[1], chosen[2]), triple)
        return gap_between(maxima.reshape(-1, H), totals.reshape(-1, H), summed.reshape(-1, H, HD), dilation)
    local_part = branch_softmax_totals(SEQUENCE_TOKENS // TOK_DEV, 1)
    group_portion = branch_softmax_totals(SEQUENCE_TOKENS // MIDDLE_SEGMENT, MIDDLE_DILATION)
    global_portion = branch_softmax_totals(1, GLOBAL_DILATION)
    result = combine([local_part, group_portion, global_portion])
    return result.reshape(SEQUENCE_TOKENS, D).astype(jnp.bfloat16)
```

```python
import functools
import math

import jax
import jax.numpy as jnp
from jax import lax
from jax.experimental import pallas as pl
from jax.experimental.pallas import tpu as pltpu
from jax.sharding import PartitionSpec as P

H = 16
HD = 128
TQ = 256
MESH = pl.DeviceIdType.MESH
SCALE2 = math.log2(math.e) / math.sqrt(HD)
BF = jnp.bfloat16
F32 = jnp.float32


def scores_of(query_tile, key_part):
    return lax.dot_general(
        query_tile, key_part, (((1,), (1,)), ((), ())), preferred_element_type=F32
    )


def weigh(scores, value_ones):
    maxima = jnp.max(scores, axis=1, keepdims=True)
    weights = jnp.exp2((scores - maxima) * SCALE2).astype(BF)
    both = jnp.dot(weights, value_ones, preferred_element_type=F32)
    summed, totals = both[:, :HD], both[:, HD:]
    return summed / totals, maxima * SCALE2 + jnp.log2(totals)


def attend(load_query, key_part, value_part, rows, save):
    value_ones = jnp.concatenate([value_part, jnp.ones_like(value_part)], axis=1)
    tiles = rows // TQ
    scores = scores_of(load_query(0), key_part)
    for tile in range(tiles):
        later = scores_of(load_query(tile + 1), key_part) if tile + 1 < tiles else None
        save(tile, *weigh(scores, value_ones))
        scores = later


def merge(one, log_one, two, log_two):
    high = jnp.maximum(log_one, log_two)
    w_one, w_two = jnp.exp2(log_one - high), jnp.exp2(log_two - high)
    total = w_one + w_two
    return (one * w_one + two * w_two) / total, high + jnp.log2(total)


def kernel(
    n_grp, n_dev, split,
    q_hbm, k_hbm, v_hbm, out_hbm, mix_hbm,
    rows_in, rows_out, wide, wide_log, picked, staged, heads_in,
    glob_out, glob_in, back_out, back_log, back_in, back_log_in, own_sum, own_log, mix,
    load_sem, store_sem, mix_sem, go_sem, come_sem, glob_go, glob_come, back_go, back_come,
):
    grp, dev = lax.axis_index("grp"), lax.axis_index("dev")
    tok = q_hbm.shape[0]
    per = tok // n_dev
    chunk = tok // 4
    glob_rows = tok // n_grp
    sources = (q_hbm, k_hbm, v_hbm)
    order = (1, 2, 0)

    def load(which, part):
        rows = pl.ds(part * chunk, chunk)
        return pltpu.make_async_copy(
            sources[which].at[rows, :], rows_in.at[which, rows, :], load_sem.at[which, part]
        )

    for which in order:
        for part in range(4):
            load(which, part).start()

    barrier = pltpu.get_barrier_semaphore()
    for step in range(1, n_dev):
        pl.semaphore_signal(
            barrier, inc=1, device_id=(grp, lax.rem(dev + step, n_dev)), device_id_type=MESH
        )
    for step in range(1, n_grp):
        pl.semaphore_signal(
            barrier, inc=1, device_id=(lax.rem(grp + step, n_grp), dev), device_id_type=MESH
        )

    def send_rows(which, peer):
        return pltpu.make_async_remote_copy(
            src_ref=staged.at[which, peer], dst_ref=heads_in.at[which, dev],
            send_sem=go_sem.at[which, peer], recv_sem=come_sem.at[which, dev],
            device_id=(grp, peer), device_id_type=MESH,
        )

    def come_rows(which, peer):
        return pltpu.make_async_remote_copy(
            src_ref=staged.at[which, peer], dst_ref=heads_in.at[which, peer],
            send_sem=go_sem.at[which, peer], recv_sem=come_sem.at[which, peer],
            device_id=(grp, peer), device_id_type=MESH,
        )

    row_ids = lax.broadcasted_iota(jnp.int32, (1, n_dev, HD), 1).astype(F32).astype(BF)
    for number, which in enumerate(order):
        for part in range(4):
            load(which, part).wait()
            chosen = None
            for head in range(H):
                piece = rows_in[
                    which, part * chunk:(part + 1) * chunk, head * HD:(head + 1) * HD
                ].reshape(chunk // n_dev, n_dev, HD)
                if chosen is None:
                    chosen = piece
                else:
                    chosen = jnp.where(row_ids == jnp.asarray(head, BF), piece, chosen)
            picked[part * chunk:(part + 1) * chunk, :] = chosen.reshape(chunk, HD).astype(F32)
        for head in range(H):
            staged[which, head] = picked[pl.ds(head, per, stride=n_dev), :].astype(BF)
        if number == 0:
            pl.semaphore_wait(barrier, n_dev - 1 + n_grp - 1)
        heads_in[which, dev] = staged[which, dev]
        for step in range(1, n_dev):
            send_rows(which, lax.rem(dev + step, n_dev)).start()

    def store(head):
        columns = pl.ds(pl.multiple_of(head * HD, HD), HD)
        return pltpu.make_async_copy(
            rows_out.at[:, columns], out_hbm.at[:, columns], store_sem.at[head]
        )

    def local_heads(first, last):
        def one(head, carry):
            columns = pl.ds(pl.multiple_of(head * HD, HD), HD)

            def load_query(tile):
                return rows_in[0, pl.ds(tile * TQ, TQ), columns]

            def save(tile, normal, logs):
                rows = pl.ds(tile * TQ, TQ)
                rows_out[rows, columns] = normal.astype(BF)
                wide[rows, :] = normal
                wide_log[rows, :] = logs

            attend(load_query, rows_in[1, :, columns], rows_in[2, :, columns], tok, save)
            own_sum[head] = wide[pl.ds(head, per, stride=n_dev), :]
            own_log[head] = wide_log[pl.ds(head, per, stride=n_dev), :]
            store(head).start()
            return carry

        lax.fori_loop(first, last, one, 0)

    local_heads(0, split[0])

    for which in (1, 2):
        for step in range(1, n_dev):
            come_rows(which, lax.rem(dev + n_dev - step, n_dev)).wait_recv()
        picked[...] = heads_in[which].reshape(tok, HD).astype(F32)
        glob_out[which - 1] = picked[pl.ds(0, glob_rows, stride=n_grp), :].astype(BF)

    def send_glob(step):
        peer = lax.rem(grp + step, n_grp)
        return pltpu.make_async_remote_copy(
            src_ref=glob_out, dst_ref=glob_in.at[:, grp],
            send_sem=glob_go.at[peer], recv_sem=glob_come.at[grp],
            device_id=(peer, dev), device_id_type=MESH,
        )

    def come_glob(step):
        peer = lax.rem(grp + n_grp - step, n_grp)
        return pltpu.make_async_remote_copy(
            src_ref=glob_out, dst_ref=glob_in.at[:, peer],
            send_sem=glob_go.at[peer], recv_sem=glob_come.at[peer],
            device_id=(peer, dev), device_id_type=MESH,
        )

    for step in range(1, n_grp):
        send_glob(step).start()
    glob_in[:, grp] = glob_out[...]

    for step in range(1, n_dev):
        come_rows(0, lax.rem(dev + n_dev - step, n_dev)).wait_recv()

    def load_middle(tile):
        part = TQ // per
        return heads_in[0, tile * part:(tile + 1) * part].reshape(TQ, HD)

    def save_middle(tile, normal, logs):
        wide[tile * TQ:(tile + 1) * TQ, :] = normal
        wide_log[tile * TQ:(tile + 1) * TQ, :] = logs

    attend(
        load_middle, heads_in[1].reshape(tok, HD), heads_in[2].reshape(tok, HD), tok, save_middle
    )
    picked[...] = heads_in[0].reshape(tok, HD).astype(F32)

    for step in range(1, n_grp):
        come_glob(step).wait_recv()
    glob_query = picked[pl.ds(0, glob_rows, stride=n_grp), :].astype(BF)
    glob_value = glob_in[1].reshape(tok, HD)
    glob_normal, glob_log = weigh(
        scores_of(glob_query, glob_in[0].reshape(tok, HD)),
        jnp.concatenate([glob_value, jnp.ones_like(glob_value)], axis=1),
    )
    which_rows = pl.ds(0, glob_rows, stride=n_grp)
    both, both_log = merge(wide[which_rows, :], wide_log[which_rows, :], glob_normal, glob_log)
    wide[which_rows, :] = both
    wide_log[which_rows, :] = both_log
    back_out[...] = wide[...].astype(BF).reshape(n_dev, per, HD)
    lanes = lax.broadcasted_iota(jnp.int32, (1, 8, HD), 2) // (HD * 8 // per)
    logs = wide_log[...].reshape(n_dev, per // 8, 8, HD)
    packed = logs[:, 0]
    for turn in range(1, per // 8):
        packed = jnp.where(lanes == turn, logs[:, turn], packed)
    back_log[...] = packed

    def send_back(step):
        peer = lax.rem(dev + step, n_dev)
        return [
            pltpu.make_async_remote_copy(
                src_ref=src.at[peer], dst_ref=dst.at[dev],
                send_sem=back_go.at[number, peer], recv_sem=back_come.at[number, dev],
                device_id=(grp, peer), device_id_type=MESH,
            )
            for number, (src, dst) in enumerate(((back_log, back_log_in), (back_out, back_in)))
        ]

    def come_back(peer):
        return [
            pltpu.make_async_remote_copy(
                src_ref=src.at[peer], dst_ref=dst.at[peer],
                send_sem=back_go.at[number, peer], recv_sem=back_come.at[number, peer],
                device_id=(grp, peer), device_id_type=MESH,
            )
            for number, (src, dst) in enumerate(((back_log, back_log_in), (back_out, back_in)))
        ]

    for step in range(1, n_dev):
        for copy in send_back(step):
            copy.start()
    back_in[dev] = back_out[dev]
    back_log_in[dev] = back_log[dev]

    local_heads(split[0], H)

    for step in range(1, n_dev):
        for copy in come_back(lax.rem(dev + n_dev - step, n_dev)):
            copy.wait_recv()
    for head in range(H):
        lane_log = back_log_in[head]
        width = HD * 8 // per
        far_log = jnp.concatenate(
            [
                jnp.broadcast_to(lane_log[:, turn * width:turn * width + 1], (8, HD))
                for turn in range(per // 8)
            ],
            axis=0,
        )
        both, _ = merge(own_sum[head], own_log[head], back_in[head].astype(F32), far_log)
        mix[:, head * HD:(head + 1) * HD] = both.astype(BF)
    out_copy = pltpu.make_async_copy(mix, mix_hbm, mix_sem)
    out_copy.start()
    for which in order:
        for step in range(1, n_dev):
            send_rows(which, lax.rem(dev + step, n_dev)).wait_send()
    for step in range(1, n_grp):
        send_glob(step).wait_send()
    for step in range(1, n_dev):
        for copy in send_back(step):
            copy.wait_send()
    for head in range(H):
        store(head).wait()
    out_copy.wait()


def body(queries, key_rows, value_rows):
    tok, width = queries.shape
    n_dev, n_grp = lax.axis_size("dev"), lax.axis_size("grp")
    per = tok // n_dev
    any_spec = pl.BlockSpec(memory_space=pl.ANY)
    dma = pltpu.SemaphoreType.DMA
    local, mix = pl.pallas_call(
        functools.partial(kernel, n_grp, n_dev, (10,)),
        out_shape=(
            jax.ShapeDtypeStruct((tok, width), BF),
            jax.ShapeDtypeStruct((per, width), BF),
        ),
        in_specs=[any_spec] * 3,
        out_specs=(any_spec, any_spec),
        scratch_shapes=[
            pltpu.VMEM((3, tok, width), BF),
            pltpu.VMEM((tok, width), BF),
            pltpu.VMEM((tok, HD), F32),
            pltpu.VMEM((tok, HD), F32),
            pltpu.VMEM((tok, HD), F32),
            pltpu.VMEM((3, n_dev, per, HD), BF),
            pltpu.VMEM((3, n_dev, per, HD), BF),
            pltpu.VMEM((2, tok // n_grp, HD), BF),
            pltpu.VMEM((2, n_grp, tok // n_grp, HD), BF),
            pltpu.VMEM((n_dev, per, HD), BF),
            pltpu.VMEM((n_dev, 8, HD), F32),
            pltpu.VMEM((n_dev, per, HD), BF),
            pltpu.VMEM((n_dev, 8, HD), F32),
            pltpu.VMEM((H, per, HD), F32),
            pltpu.VMEM((H, per, HD), F32),
            pltpu.VMEM((per, width), BF),
            dma((3, 4)),
            dma((H,)),
            dma,
            dma((3, n_dev)),
            dma((3, n_dev)),
            dma((n_grp,)),
            dma((n_grp,)),
            dma((2, n_dev)),
            dma((2, n_dev)),
        ],
        compiler_params=pltpu.CompilerParams(
            collective_id=0, has_side_effects=True, vmem_limit_bytes=60 << 20
        ),
    )(queries, key_rows, value_rows)
    shape = (per, n_dev, H, HD)
    chosen = lax.broadcasted_iota(jnp.int32, (per, n_dev, width), 1) == (
        lax.broadcasted_iota(jnp.int32, (per, n_dev, width), 2) // HD
    )
    return jnp.where(
        chosen, mix[:, None, :], local.reshape(per, n_dev, width)
    ).reshape(tok, width)


def solution(mesh):
    spec = P(("grp", "dev"), None)
    return jax.shard_map(
        body, mesh=mesh, in_specs=(spec, spec, spec), out_specs=spec, check_vma=False
    )
```
